32 devices in a mesh: section: 2 (over y), expert: 8 (over z, x), dp: 2 (over core).
Axes of the slice: x: 2, y: 2, z: 4, core: 2. Of those that a mesh axis runs over, the one named last changes fastest.
Arguments:
- tokens_in: bfloat16 [8, 256, 2048], P(None, ('expert', 'dp')), may hold values from -6 to 6
- cotangent: bfloat16 [8, 256, 2048], P(None, ('expert', 'dp')), may hold values from -4 to 4
- routes: int32 [2, 8, 256, 8], P('section', None, ('expert', 'dp')), may hold values from 0 to 15, all different within a row; in each aligned block of 16 rows (0 to 15, 16 to 31, ..., all dimensions but the last counted through in order) at most 10 rows name the same one
- router_weights: float32 [2, 8, 256, 8], P('section', None, ('expert', 'dp')), may hold values from 0.1 to 0.6
- norm_gain: float32 [2, 2048], P('section'), may hold values from 0.25 to 1.75
- w_gate: bfloat16 [2, 16, 2048, 512], P('section', 'expert'), may hold values from -0.125 to 0.125
- w_up: bfloat16 [2, 16, 2048, 512], P('section', 'expert'), may hold values from -0.125 to 0.125
- w_down: bfloat16 [2, 16, 512, 2048], P('section', 'expert'), may hold values from -0.25 to 0.25
Outputs:
- layer_out: bfloat16 [2, 8, 256, 2048], P('section', None, ('expert', 'dp'))
- input_grad: bfloat16 [2, 8, 256, 2048], P('section', None, ('expert', 'dp'))
- grad_gate: bfloat16 [2, 16, 2048, 512], P('section', 'expert', 'dp')
- grad_up: bfloat16 [2, 16, 2048, 512], P('section', 'expert', 'dp')
- grad_down: bfloat16 [2, 16, 512, 2048], P('section', 'expert', 'dp')
The draws below stay inside these ranges and needn't reach their ends.
Inputs may be any that keep to these rules, and one draw needn't show every extreme that they name: `routes`: each row names 8 different experts. In each aligned block of 16 rows (the tokens of one device for one layer and one micro-batch) no expert is named by more than 10 rows, and in some blocks one is named by exactly 10.
All inputs are finite; a program needn't handle non-finite values.
Results may differ from the reference program's by a relative error of at most 0.022.
Values may be sent and summed in bfloat16 or wider, within the bound.
A program may use at most 128 MiB of HBM per device.

```python
import math
import jax
import jax.numpy as jnp
import numpy as np
from jax import lax

D = 2048
FF = 512
TOP = 8
MICRO = 8
TOK_MB = 16
SECTIONS = 2
EXPERTS = 16
TOKENS = 256
CAP = 10
N_EXPERT = 8
N_DP = 2


def levels(rng, extent, cuts, low, top_value):
    def one(dim, shards_of):
        heights = jax.random.uniform(jax.random.fold_in(jax.random.fold_in(rng, 6), dim), (shards_of,), jnp.float32, low / len(cuts), top_value / len(cuts))
        return jnp.repeat(jnp.exp(heights), extent[dim] // shards_of).reshape((-1,) + (1,) * (len(extent) - dim - 1))

    level = one(*cuts[0])
    for cut in cuts[1:]:
        level = level * one(*cut)
    return level


def shared_out(key, own, number, rows, amount, top, reach, skew):
    sequence = jax.random.permutation(key, amount)
    heavy_load, common = portions_of(amount, rows * top, reach, skew, True), portions_of(amount, rows * top, reach, skew, False)
    places = jnp.arange(amount)

    def named(lengths, turn):
        used = int((lengths > 0).sum())
        fixed = max(1, used // 4)
        passed = fixed + (places - fixed + turn * (used - fixed)) % max(1, amount - fixed)
        return jnp.zeros((amount,), jnp.int32).at[sequence[jnp.where(places < fixed, places, passed)]].set(jnp.asarray(lengths, jnp.int32))

    lengths = jnp.where(number % 4 == 0, named(heavy_load, number // 4), named(common, number - number // 4 - 1))
    mixed = jax.random.permutation(jax.random.fold_in(own, 3), amount)
    source_of, receiver = mixed[0:amount // 2 * 2:2], mixed[1:amount // 2 * 2:2]
    room = jnp.minimum(lengths[source_of] - 1, reach - lengths[receiver]) // 2
    room = jnp.where((source_of == sequence[0]) | (receiver == sequence[0]) | (lengths[receiver] == 0), 0, jnp.maximum(room, 0))
    passed = jax.random.randint(jax.random.fold_in(own, 4), (amount // 2,), 0, 1 << 20) % (room + 1)
    lengths = lengths.at[source_of].add(-passed).at[receiver].add(passed)
    items = jnp.searchsorted(jnp.cumsum(lengths), jnp.arange(rows * top), side="right").astype(jnp.int32)
    listing = items.reshape(top, rows).T
    listing = listing[jax.random.permutation(jax.random.fold_in(own, 1), rows)]
    turn = jax.random.randint(jax.random.fold_in(own, 2), (rows, 1), 0, top)
    return jnp.take_along_axis(listing, (jnp.arange(top)[None, :] + turn) % top, axis=1)


def portions_of(amount, total, reach, skew, full):
    portions = [(1 << 20) // math.isqrt(standing ** skew) + 1 for standing in range(1, amount + 1)]
    largest = reach if full else min(reach, max(-(-total // amount), total * portions[0] // sum(portions)))
    least = 1 if total - largest >= amount - 1 else 0
    given, rest = [largest] + [least] * (amount - 1), total - largest - least * (amount - 1)
    while rest > 0:
        candidates = [i for i in range(1, amount) if given[i] < largest] or [i for i in range(1, amount) if given[i] < reach]
        whole, left = sum([portions[i] for i in candidates]), rest
        for i in candidates:
            addition = min(reach - given[i], max(1, left * portions[i] // whole), rest)
            given[i] = given[i] + addition
            rest = rest - addition
    return np.array(given)


def bell_draw(key, dims, spread, bound, cuts=(), kind=jnp.bfloat16):
    level = levels(key, dims, cuts, -0.22, 0.18) if cuts else 1.0
    result = jax.random.normal(key, dims, jnp.float32) * spread * level
    return jnp.minimum(jnp.maximum(result, -bound), bound).astype(kind)


def setup_inputs(seed: int = 0) -> dict:
    splits = jax.random.split(jax.random.key(seed), 9)
    tokens_in = bell_draw(splits[0], (MICRO, TOKENS, D), 1.0, 6.0, ((1, 16),))
    cotangent = bell_draw(splits[1], (MICRO, TOKENS, D), 0.25, 4.0, ((1, 16),))
    routes_keys = jax.random.split(jax.random.fold_in(splits[2], 1), SECTIONS * MICRO * TOKENS // TOK_MB)
    routes_turns = jax.random.permutation(jax.random.fold_in(splits[2], 3), SECTIONS * MICRO * TOKENS // TOK_MB)
    routes = jax.vmap(lambda own, number: shared_out(jax.random.fold_in(splits[2], 2), own, number, TOK_MB, EXPERTS, TOP, CAP, 1))(routes_keys, routes_turns).reshape((SECTIONS, MICRO, TOKENS, TOP))
    router_weights = jnp.clip(jnp.exp(math.log(0.6) - 1.7917595 * jax.random.uniform(splits[3], (SECTIONS, MICRO, TOKENS, TOP), jnp.float32) ** levels(splits[3], (SECTIONS, MICRO, TOKENS, TOP), ((0, 2), (2, 16)), -0.2, 0.2)), 0.1, 0.6)
    norm_gain = jnp.clip(1.0 + 0.15 * jax.random.normal(splits[4], (SECTIONS, D), jnp.float32), 0.25, 1.75)
    w_gate = bell_draw(splits[5], (SECTIONS, EXPERTS, D, FF), D ** -0.5, 0.125, ((0, 2), (1, 8)))
    w_up = bell_draw(splits[6], (SECTIONS, EXPERTS, D, FF), D ** -0.5, 0.125, ((0, 2), (1, 8)))
    w_down = bell_draw(splits[7], (SECTIONS, EXPERTS, FF, D), FF ** -0.5, 0.25, ((0, 2), (1, 8)))
    return {"tokens_in": tokens_in, "cotangent": cotangent, "routes": routes, "router_weights": router_weights, "norm_gain": norm_gain, "w_gate": w_gate, "w_up": w_up, "w_down": w_down}


epsilon = 1e-06

def normalize(hidden, gain_row):
    widened = hidden.astype(jnp.float32)
    inv_rms = lax.rsqrt(lax.optimization_barrier(jnp.mean(widened * widened, axis=-1, keepdims=True)) + epsilon)
    return ((widened * inv_rms * gain_row).astype(jnp.bfloat16), widened, inv_rms)

def slot_rows(route_ids):
    blocks = N_EXPERT * N_DP
    per_block = TOK_MB * TOP
    grouped = route_ids.reshape(MICRO, blocks, per_block)
    labels = jnp.arange(EXPERTS, dtype=jnp.int32)
    onehot = (grouped[:, :, :, None] == labels).astype(jnp.int32)
    earlier = jnp.cumsum(onehot, axis=2) - onehot
    position = lax.optimization_barrier(jnp.sum(earlier * onehot, axis=3)).astype(jnp.int32)
    block_ids = jnp.arange(MICRO, dtype=jnp.int32)[:, None, None] * blocks + jnp.arange(blocks, dtype=jnp.int32)[None, :, None]
    expert_rows = MICRO * blocks * CAP
    flat_rows = grouped * expert_rows + block_ids * CAP + position
    return flat_rows.reshape(MICRO * TOKENS * TOP).astype(jnp.int32)

def source_table(flat_rows):
    total = MICRO * TOKENS * TOP
    expert_rows = MICRO * N_EXPERT * N_DP * CAP
    source = jnp.full((EXPERTS * expert_rows,), total, dtype=jnp.int32)
    source = source.at[flat_rows].set(jnp.arange(total, dtype=jnp.int32))
    return source.reshape(EXPERTS, expert_rows)

def layer_forward(hidden, route_ids, route_weights, gain_row, gate_w, up_w, down_w):
    normed, widened, inv_rms = normalize(hidden, gain_row)
    flat_rows = slot_rows(route_ids)
    source = source_table(flat_rows)
    padded = jnp.concatenate([normed.reshape(MICRO * TOKENS, D), jnp.zeros((1, D), jnp.bfloat16)], axis=0)

    def one_expert(inputs):
        picks, gate_m, up_m, down_m = inputs
        rows_in = padded[picks // TOP]
        gate_pre = jnp.dot(rows_in, gate_m, preferred_element_type=jnp.float32)
        up_pre = jnp.dot(rows_in, up_m, preferred_element_type=jnp.float32)
        act_value = (jax.nn.silu(gate_pre) * up_pre).astype(jnp.bfloat16)
        return jnp.dot(act_value, down_m, preferred_element_type=jnp.float32).astype(jnp.bfloat16)
    produced = lax.map(one_expert, (source, gate_w, up_w, down_w))
    gathered = produced.reshape(EXPERTS * source.shape[1], D)[flat_rows].astype(jnp.float32)
    gathered = gathered.reshape(MICRO, TOKENS, TOP, D)
    mixed_sum = widened + lax.optimization_barrier(jnp.sum(route_weights[:, :, :, None] * gathered, axis=2))
    return mixed_sum.astype(jnp.bfloat16)

def round_part(partial_value):
    return lax.optimization_barrier(partial_value.astype(jnp.bfloat16)).astype(jnp.float32)

def layer_backward(hidden, grad_out, route_ids, route_weights, gain_row, gate_w, up_w, down_w):
    normed, widened, inv_rms = normalize(hidden, gain_row)
    flat_rows = slot_rows(route_ids)
    source = source_table(flat_rows)
    total = MICRO * TOKENS * TOP
    padded = jnp.concatenate([normed.reshape(MICRO * TOKENS, D), jnp.zeros((1, D), jnp.bfloat16)], axis=0)
    spread_grad = route_weights.reshape(MICRO * TOKENS, TOP)[:, :, None] * grad_out.reshape(MICRO * TOKENS, 1, D).astype(jnp.float32)
    padded_grad = jnp.concatenate([spread_grad.astype(jnp.bfloat16).reshape(total, D), jnp.zeros((1, D), jnp.bfloat16)], axis=0)
    split_shape = (MICRO, N_EXPERT, N_DP, CAP)

    def one_expert(inputs):
        picks, gate_m, up_m, down_m = inputs
        rows_in = padded[picks // TOP]
        out_grad = padded_grad[picks]
        gate_pre = jnp.dot(rows_in, gate_m, preferred_element_type=jnp.float32)
        up_pre = jnp.dot(rows_in, up_m, preferred_element_type=jnp.float32)
        sigmoid_g = jax.nn.sigmoid(gate_pre)
        act_value = (jax.nn.silu(gate_pre) * up_pre).astype(jnp.bfloat16)
        act_grad = jnp.dot(out_grad, down_m.T, preferred_element_type=jnp.float32)
        up_grad = (act_grad * gate_pre * sigmoid_g).astype(jnp.bfloat16)
        gate_grad = (act_grad * up_pre * sigmoid_g * (1.0 + gate_pre * (1.0 - sigmoid_g))).astype(jnp.bfloat16)
        row_grad = (jnp.dot(gate_grad, gate_m.T, preferred_element_type=jnp.float32) + jnp.dot(up_grad, up_m.T, preferred_element_type=jnp.float32)).astype(jnp.bfloat16)
        rows_split = rows_in.reshape(split_shape + (D,))
        gate_split = gate_grad.reshape(split_shape + (FF,))
        up_split = up_grad.reshape(split_shape + (FF,))
        act_split = act_value.reshape(split_shape + (FF,))
        out_split = out_grad.reshape(split_shape + (D,))
        gate_total = jnp.zeros((D, FF), jnp.float32)
        up_total = jnp.zeros((D, FF), jnp.float32)
        down_total = jnp.zeros((FF, D), jnp.float32)
        for data_index in range(N_DP):
            part_rows = rows_split[:, :, data_index].reshape(-1, D)
            part_act = act_split[:, :, data_index].reshape(-1, FF)
            gate_total = gate_total + round_part(jnp.dot(part_rows.T, gate_split[:, :, data_index].reshape(-1, FF), preferred_element_type=jnp.float32))
            up_total = up_total + round_part(jnp.dot(part_rows.T, up_split[:, :, data_index].reshape(-1, FF), preferred_element_type=jnp.float32))
            down_total = down_total + round_part(jnp.dot(part_act.T, out_split[:, :, data_index].reshape(-1, D), preferred_element_type=jnp.float32))
        return (row_grad, gate_total.astype(jnp.bfloat16), up_total.astype(jnp.bfloat16), down_total.astype(jnp.bfloat16))
    row_grads, gate_grads, up_grads, down_grads = lax.map(one_expert, (source, gate_w, up_w, down_w))
    backed = row_grads.reshape(EXPERTS * source.shape[1], D)[flat_rows].astype(jnp.float32)
    dnormed = lax.optimization_barrier(jnp.sum(backed.reshape(MICRO, TOKENS, TOP, D), axis=2))
    scaled = dnormed * gain_row
    unit_rows = widened * inv_rms
    dhidden = grad_out.astype(jnp.float32) + inv_rms * (scaled - unit_rows * lax.optimization_barrier(jnp.mean(scaled * unit_rows, axis=-1, keepdims=True)))
    return (dhidden.astype(jnp.bfloat16), gate_grads, up_grads, down_grads)

def reference(tokens_in, cotangent, routes, router_weights, norm_gain, w_gate, w_up, w_down):
    hidden = tokens_in
    layer_inputs = []
    layer_outputs = []
    for layer_index in range(SECTIONS):
        layer_inputs.append(hidden)
        hidden = layer_forward(hidden, routes[layer_index], router_weights[layer_index], norm_gain[layer_index], w_gate[layer_index], w_up[layer_index], w_down[layer_index])
        layer_outputs.append(hidden)
    gradient = cotangent
    input_grads = [None] * SECTIONS
    gate_list = [None] * SECTIONS
    up_list = [None] * SECTIONS
    down_list = [None] * SECTIONS
    for layer_index in reversed(range(SECTIONS)):
        gradient, gate_part, up_part, down_part = layer_backward(layer_inputs[layer_index], gradient, routes[layer_index], router_weights[layer_index], norm_gain[layer_index], w_gate[layer_index], w_up[layer_index], w_down[layer_index])
        input_grads[layer_index] = gradient
        gate_list[layer_index] = gate_part
        up_list[layer_index] = up_part
        down_list[layer_index] = down_part
    return (jnp.stack(layer_outputs), jnp.stack(input_grads), jnp.stack(gate_list), jnp.stack(up_list), jnp.stack(down_list))
```

```python
import jax
import jax.numpy as jnp
from jax import lax
from jax.sharding import PartitionSpec as P

epsilon = 1e-06
ROW_LIMIT = 1024


def from_behind(block, axis, distance):
    devices = range(lax.axis_size(axis))
    route = [(i - distance, i) for i in devices if i - distance in devices]
    return lax.ppermute(block, axis, route)


def pick(section_id, by_section):
    entries = list(by_section.items())
    chosen = entries[0][1]
    for section, value in entries[1:]:
        if value is not chosen:
            chosen = jnp.where(section_id == section, value, chosen)
    return chosen


def weight_table(route_ids, route_weights, experts, expert_count):
    labels = jnp.arange(experts, dtype=jnp.int32)[:, None, None, None]
    dense = jnp.sum(jnp.where(route_ids[None] == labels, route_weights[None], 0.0), axis=3)
    dense = dense.reshape((expert_count, experts // expert_count) + dense.shape[1:])
    return lax.all_to_all(dense, "expert", split_axis=0, concat_axis=0, tiled=True)


def on_device(tokens_in, cotangent, routes, router_weights, norm_gain, w_gate, w_up, w_down):
    micro_count, token_rows, width = tokens_in.shape
    held, hidden_units = w_gate.shape[1], w_gate.shape[3]
    sections = lax.axis_size("section")
    expert_count = lax.axis_size("expert")
    dp_count = lax.axis_size("dp")
    chunks = 1
    while micro_count % (2 * chunks) == 0 and micro_count * token_rows * expert_count > ROW_LIMIT * chunks:
        chunks *= 2
    per_chunk = micro_count // chunks
    own_rows = per_chunk * token_rows
    ticks = sections + chunks - 1
    inner = held * hidden_units
    section_id = lax.axis_index("section")
    gain_row = norm_gain[0]
    table = weight_table(routes[0], router_weights[0], held * expert_count, expert_count)
    w_in = jnp.concatenate([w_gate[0, e] for e in range(held)] + [w_up[0, e] for e in range(held)], axis=1)
    w_out = w_down[0].reshape(inner, width)

    def chunk_of(array, chunk, axis):
        if chunks == 1:
            return array
        return lax.dynamic_slice_in_dim(array, chunk * per_chunk, per_chunk, axis)

    def spread_weights(chunk):
        rows = chunk_of(table, chunk, 2).transpose(0, 2, 3, 1).reshape(-1, held)
        return jnp.repeat(rows, hidden_units, axis=1)

    def gather(rows):
        return lax.all_gather(rows, "expert", axis=0, tiled=True)

    def scatter(rows):
        return lax.psum_scatter(rows, "expert", scatter_dimension=0, tiled=True)

    def rms(hidden):
        widened = hidden.astype(jnp.float32)
        return widened, lax.rsqrt(jnp.mean(widened * widened, axis=-1, keepdims=True) + epsilon)

    compact = sections > 2

    def keep(store, value, owner):
        if not compact:
            store.append(value)
        elif not store:
            store.extend([value] * chunks)
        else:
            store[:] = [jnp.where(section_id == owner(c), value, old) for c, old in enumerate(store)]
            store[:] = lax.optimization_barrier(store)

    def at(store, chunk, shift):
        return store[chunk] if compact else store[chunk + shift]

    hiddens, rows_in, pre_acts, acts, outputs = [], [], [], [], []
    incoming = None
    for tick in range(ticks):
        chunk = jnp.clip(tick - section_id, 0, chunks - 1)
        hidden = None
        if tick < chunks:
            hidden = chunk_of(tokens_in, chunk, 0).reshape(own_rows, width)
        if tick > 0:
            hidden = incoming if hidden is None else jnp.where(section_id == 0, hidden, incoming)
        widened, inv_rms = rms(hidden)
        gathered = gather((widened * inv_rms * gain_row).astype(jnp.bfloat16))
        pre = jnp.dot(gathered, w_in, preferred_element_type=jnp.float32).astype(jnp.bfloat16)
        gate, up = pre[:, :inner].astype(jnp.float32), pre[:, inner:].astype(jnp.float32)
        act = (gate * jax.nn.sigmoid(gate) * up * spread_weights(chunk)).astype(jnp.bfloat16)
        mixed = jnp.dot(act, w_out, preferred_element_type=jnp.float32).astype(jnp.bfloat16)
        output = (widened + scatter(mixed).astype(jnp.float32)).astype(jnp.bfloat16)
        if tick < ticks - 1:
            incoming = from_behind(output, "section", 1)
        keep(hiddens, hidden, lambda c: tick - c)
        keep(rows_in, gathered, lambda c: tick - c)
        keep(pre_acts, pre, lambda c: tick - c)
        keep(acts, act, lambda c: tick - c)
        keep(outputs, output, lambda c: tick - c)

    grads_in, pre_grads, results = [], [], []
    for tick in range(ticks):
        chunk = jnp.clip(tick - (sections - 1 - section_id), 0, chunks - 1)
        active = {
            s: tick - (sections - 1 - s)
            for s in range(sections)
            if 0 <= tick - (sections - 1 - s) < chunks
        }
        grad_out = None
        if tick < chunks:
            grad_out = chunk_of(cotangent, chunk, 0).reshape(own_rows, width)
        if tick > 0:
            grad_out = incoming if grad_out is None else jnp.where(section_id == sections - 1, grad_out, incoming)
        gathered = gather(grad_out)
        pre = pick(section_id, {s: at(pre_acts, c, s) for s, c in active.items()})
        gate, up = pre[:, :inner].astype(jnp.float32), pre[:, inner:].astype(jnp.float32)
        act_grad = lax.dot_general(
            gathered, w_out, (((1,), (1,)), ((), ())), preferred_element_type=jnp.float32
        )
        act_grad = act_grad * spread_weights(chunk)
        sig = jax.nn.sigmoid(gate)
        pre_grad = jnp.concatenate(
            [
                (act_grad * up * sig * (1.0 + gate * (1.0 - sig))).astype(jnp.bfloat16),
                (act_grad * gate * sig).astype(jnp.bfloat16),
            ],
            axis=1,
        )
        row_grad = lax.dot_general(
            pre_grad, w_in, (((1,), (1,)), ((), ())), preferred_element_type=jnp.float32
        ).astype(jnp.bfloat16)
        dnormed = scatter(row_grad).astype(jnp.float32)
        hidden = pick(section_id, {s: at(hiddens, c, s) for s, c in active.items()})
        widened, inv_rms = rms(hidden)
        unit = widened * inv_rms
        scaled = dnormed * gain_row
        result = (
            grad_out.astype(jnp.float32)
            + inv_rms * (scaled - unit * jnp.mean(scaled * unit, axis=-1, keepdims=True))
        ).astype(jnp.bfloat16)
        if tick < ticks - 1:
            incoming = from_behind(result, "section", -1)
        keep(grads_in, gathered, lambda c: sections - 1 - tick + c)
        keep(pre_grads, pre_grad, lambda c: sections - 1 - tick + c)
        keep(results, result, lambda c: sections - 1 - tick + c)

    def contract(left, right):
        return lax.dot_general(left, right, (((0,), (0,)), ((), ())), preferred_element_type=jnp.float32)

    def summed(pairs):
        total = contract(*pairs[0])
        for pair in pairs[1:]:
            total = total + contract(*pair)
        return total.astype(jnp.bfloat16)


    def split_columns(array, groups, part):
        size = array.shape[1] // groups
        piece = size // dp_count
        cuts = [lax.dynamic_slice_in_dim(array, g * size + part * piece, piece, 1) for g in range(groups)]
        return cuts[0] if groups == 1 else jnp.concatenate(cuts, axis=1)

    def in_weight_part(part):
        def branch(section):
            back = sections - 1 - section
            return lambda: summed(
                [(split_columns(at(rows_in, c, section), 1, part), at(pre_grads, c, back)) for c in range(chunks)]
            )

        if compact:
            return branch(0)()
        return lax.switch(section_id, [branch(s) for s in range(sections)])

    def out_weight_part(part):
        def branch(section):
            back = sections - 1 - section
            return lambda: summed(
                [(split_columns(at(acts, c, section), held, part), at(grads_in, c, back)) for c in range(chunks)]
            )

        if compact:
            return branch(0)()
        return lax.switch(section_id, [branch(s) for s in range(sections)])

    dp_id = lax.axis_index("dp")

    def over_dp(part_fn):
        total = part_fn(dp_id).astype(jnp.float32)
        for distance in range(1, dp_count):
            ring = [(i, (i + distance) % dp_count) for i in range(dp_count)]
            other = part_fn((dp_id + distance) % dp_count)
            total = total + lax.ppermute(other, "dp", ring).astype(jnp.float32)
        return total.astype(jnp.bfloat16)

    out_grads = over_dp(out_weight_part)
    in_grads = over_dp(in_weight_part)
    grad_gate = jnp.stack([in_grads[:, e * hidden_units : (e + 1) * hidden_units] for e in range(held)])
    grad_up = jnp.stack([in_grads[:, inner + e * hidden_units : inner + (e + 1) * hidden_units] for e in range(held)])
    grad_down = out_grads.reshape(held, hidden_units // dp_count, width)

    def in_order(per_tick, first_tick):
        kept = pick(
            section_id,
            {
                s: jnp.concatenate([at(per_tick, c, first_tick(s)) for c in range(chunks)], axis=0)
                for s in range(sections)
            },
        )
        return kept.reshape(1, micro_count, token_rows, width)

    layer_out = in_order(outputs, lambda s: s)
    input_grad = in_order(results, lambda s: sections - 1 - s)
    return (layer_out, input_grad, grad_gate[None], grad_up[None], grad_down[None])


def solution(mesh):
    placed = (
        P(None, ("expert", "dp"), None),
        P(None, ("expert", "dp"), None),
        P("section", None, ("expert", "dp"), None),
        P("section", None, ("expert", "dp"), None),
        P("section", None),
        P("section", "expert", None, None),
        P("section", "expert", None, None),
        P("section", "expert", None, None),
    )
    return jax.shard_map(
        on_device,
        mesh=mesh,
        in_specs=placed,
        out_specs=(
            P("section", None, ("expert", "dp"), None),
            P("section", None, ("expert", "dp"), None),
            P("section", "expert", "dp", None),
            P("section", "expert", "dp", None),
            P("section", "expert", "dp", None),
        ),
        check_vma=False,
    )
```
